32 devices in a mesh: dp: 8 (over z, x), ctx: 4 (over y, core).
Axes of the slice: x: 2, y: 2, z: 4, core: 2. Of those that a mesh axis runs over, the one named last changes fastest.
Arguments:
- stream: bfloat16 [8, 512, 4096], P('dp', 'ctx'), may hold values from -6 to 6
- queries: bfloat16 [8, 512, 2048], P('dp', 'ctx'), may hold values from -150 to 150
- keys: bfloat16 [8, 512, 512], P('dp', 'ctx'), may hold values from -6 to 6
- values: bfloat16 [8, 512, 512], P('dp', 'ctx'), may hold values from -6 to 6
- clip_lengths: int32 [8], P('dp'), may hold values from 256 to 512, as said below
- mod_shift: float32 [8, 4096], P('dp'), may hold values from -3 to 3
- mod_scale: float32 [8, 4096], P('dp'), may hold values from -0.5 to 0.5
- out_weight: bfloat16 [2048, 4096], P('ctx', 'dp'), may hold values from -2 to 2
- final_weight: bfloat16 [4096, 128], replicated, may hold values from -0.09375 to 0.09375
- noisy_latents: bfloat16 [8, 512, 128], P('dp', 'ctx'), may hold values from -6 to 6
- timestep: int32 [8], P('dp'), may hold values from 100 to 599
- crop_map: int32 [8, 256], P('dp'), may hold values from 0 to 511, as said below
- embed_weight: bfloat16 [128, 1408], replicated, may hold values from -0.5 to 0.5
- pre_gain: float32 [1408], replicated, may hold values from 0.1 to 1.9
- up_weight: bfloat16 [1408, 6144], P(None, 'ctx'), may hold values from -0.15625 to 0.15625
- down_weight: bfloat16 [6144, 1408], P('ctx'), may hold values from -0.21875 to 0.21875
- post_gain: float32 [1408], replicated, may hold values from 0.1 to 1.9
- head_weight: float32 [1408], replicated, may hold values from -4 to 4
Outputs:
- reward: float32 [8], P('dp')
- grad_stream: bfloat16 [8, 512, 4096], P('dp', 'ctx')
- grad_queries: bfloat16 [8, 512, 2048], P('dp', 'ctx')
The draws below stay inside these ranges and needn't reach their ends.
Inputs may be any that keep to these rules, and one draw needn't show every extreme that they name: `clip_lengths`: each clip's length lies between 256 and 512; in every draw some clip has length exactly 512. `crop_map`: every crop token of clip b points below clip_lengths[b].
All inputs are finite; a program needn't handle non-finite values.
Results may differ from the reference program's by a relative error of at most 0.04.
Values may be sent and summed in bfloat16 or wider, within the bound.
A program may use at most 128 MiB of HBM per device.

```python
import math
import jax
import jax.numpy as jnp
from jax import lax

D = 4096
HEADS = 16
KV_HEADS = 4
HEAD = 128
PATCH = 128
RW = 1408
RFF = 6144
S = 512
BATCH = 8
ROWS = 256


def attention_fields(key):
    folded = jax.random.fold_in(key, 11)
    key_rows = jax.random.truncated_normal(jax.random.fold_in(folded, 1), -6.0, 6.0, (BATCH, S, KV_HEADS * HEAD), jnp.float32)
    query_rows = jax.random.truncated_normal(jax.random.fold_in(folded, 2), -6.0, 6.0, (BATCH, S, HEADS * HEAD), jnp.float32)
    return (query_rows, key_rows)


def draw_queries(key, part):
    return attention_fields(key)[0].astype(jnp.bfloat16)


def draw_keys(key, part):
    return attention_fields(key)[1].astype(jnp.bfloat16)


def length_draw(key):
    folded = jax.random.fold_in(key, 23)
    lengths = jax.random.randint(jax.random.fold_in(folded, 1), (BATCH,), S // 2, S + 1)
    longest = jax.random.randint(jax.random.fold_in(folded, 2), (), 0, BATCH)
    return jnp.where(jnp.arange(BATCH) == longest, S, lengths).astype(jnp.int32)


def draw_clip_lengths(key, part):
    return length_draw(key)


def draw_crop_map(key, part):
    lengths = length_draw(key)
    picks = jax.random.randint(jax.random.fold_in(key, 29), (BATCH, ROWS), 0, S)
    return (picks % lengths[:, None]).astype(jnp.int32)


def with_ends(drawn, key, low, top_value):
    index_at = [jax.random.randint(jax.random.fold_in(key, axis), (), 0, length) for axis, length in enumerate(drawn.shape)]
    widest = drawn.shape.index(max(drawn.shape))
    beside = index_at[:widest] + [(index_at[widest] + 1) % drawn.shape[widest]] + index_at[widest + 1:]
    return drawn.at[tuple(index_at)].set(low).at[tuple(beside)].set(top_value)


def with_spikes(drawn, key, source, target, parts, factor):
    def block_of(position):
        return (jnp.arange(drawn.shape[position]) // (drawn.shape[position] // parts)).reshape((-1,) + (1,) * (drawn.ndim - 1 - position))

    first = jax.random.permutation(key, parts)[block_of(target)]
    second = (block_of(target) + parts // 2) % parts
    return jnp.where((block_of(source) == first) | (block_of(source) == second), factor * drawn, drawn)


def levels(stream_key, dims, cuts, low, high):
    def one(position, blocks):
        steps = jax.random.uniform(jax.random.fold_in(jax.random.fold_in(stream_key, 6), position), (blocks,), jnp.float32, low / len(cuts), high / len(cuts))
        return jnp.repeat(jnp.exp(steps), dims[position] // blocks).reshape((-1,) + (1,) * (len(dims) - position - 1))

    gain = one(*cuts[0])
    for cut in cuts[1:]:
        gain = gain * one(*cut)
    return gain


def gaussian(key, shape, scale, limit, split=(), kind=jnp.bfloat16):
    gain = levels(key, shape, split, -0.22, 0.18) if split else 1.0
    entries = jax.random.normal(key, shape, jnp.float32) * scale * gain
    return jnp.minimum(jnp.maximum(entries, -limit), limit).astype(kind)


def bell_draw_with(stream_key, extent, deviation, bound, shards, heavy, kind=jnp.bfloat16):
    entries = deviation * jax.random.normal(stream_key, extent, jnp.float32)
    if shards:
        entries = entries * levels(stream_key, extent, shards, -0.22, 0.18)
    return jnp.clip(with_spikes(entries, jax.random.fold_in(stream_key, 3), *heavy), -bound, bound).astype(kind)


def setup_inputs(seed: int = 0) -> dict:
    key_of = jax.random.split(jax.random.key(seed), 19)
    stream = gaussian(key_of[0], (BATCH, S, D), 1.0, 6.0, ((0, 8), (1, 4)))
    queries = draw_queries(jax.random.fold_in(key_of[18], 71), 0)
    keys = draw_keys(jax.random.fold_in(key_of[18], 71), 0)
    values = gaussian(key_of[3], (BATCH, S, KV_HEADS * HEAD), 1.0, 6.0, ((0, 8), (1, 4)))
    clip_lengths = draw_clip_lengths(jax.random.fold_in(key_of[18], 71), 0)
    mod_shift = gaussian(key_of[5], (BATCH, D), 0.5, 3.0, ((0, 8),), jnp.float32)
    mod_scale = jnp.clip(jax.random.uniform(key_of[6], (BATCH, D), jnp.float32, -0.5, 0.5) * levels(key_of[6], (BATCH, D), ((0, 8),), -0.4, 0.0), -0.5, 0.5)
    out_weight = gaussian(key_of[7], (HEADS * HEAD, D), (max(1, 2 * HEADS * HEAD // S)) ** -0.5, 2.0, ((0, 4), (1, 8)))
    final_weight = gaussian(key_of[8], (D, PATCH), D ** -0.5, 0.09375)
    noisy_latents = gaussian(key_of[9], (BATCH, S, PATCH), 1.0, 6.0, ((0, 8), (1, 4)))
    timestep = with_ends(jax.random.randint(key_of[10], (BATCH,), 100, 600), jax.random.fold_in(key_of[10], 1), 100, 599).astype(jnp.int32)
    crop_map = draw_crop_map(jax.random.fold_in(key_of[18], 71), 0)
    embed_weight = gaussian(key_of[12], (PATCH, RW), PATCH ** -0.5, 0.5)
    pre_gain = jnp.clip(1.0 + 0.18 * jax.random.normal(key_of[13], (RW,), jnp.float32), 0.1, 1.9)
    up_weight = gaussian(key_of[14], (RW, RFF), RW ** -0.5, 0.15625, ((1, 4),))
    down_weight = bell_draw_with(key_of[15], (RFF, RW), (RFF // 4) ** -0.5, 0.21875, ((0, 4),), (0, 1, 4, 2.0))
    post_gain = jnp.clip(1.0 + 0.18 * jax.random.normal(key_of[16], (RW,), jnp.float32), 0.1, 1.9)
    head_weight = gaussian(key_of[17], (RW,), 1.0, 4.0, (), jnp.float32)
    return dict(stream=stream, queries=queries, keys=keys, values=values, clip_lengths=clip_lengths, mod_shift=mod_shift, mod_scale=mod_scale, out_weight=out_weight, final_weight=final_weight, noisy_latents=noisy_latents, timestep=timestep, crop_map=crop_map, embed_weight=embed_weight, pre_gain=pre_gain, up_weight=up_weight, down_weight=down_weight, post_gain=post_gain, head_weight=head_weight)


MASKED = -1e+30
LOSS_SCALE = 16.0
EPSILON = 1e-06

def rounded(amount):
    return lax.optimization_barrier(amount.astype(jnp.bfloat16)).astype(jnp.float32)

def plan(noise_step):
    phase = (noise_step.astype(jnp.float32) / 1000.0 + 0.008) / 1.008 * (math.pi / 2.0)
    signal_root = jnp.cos(phase)
    return (signal_root, jnp.sqrt(1.0 - signal_root * signal_root))

def gelu_slope(hidden, upstream):
    return jax.vjp(lambda argument: jax.nn.gelu(argument, approximate=True), hidden)[1](upstream)[0]

def reward_model(crop_tokens, embed_weight, pre_gain, up_weight, down_weight, post_gain, head_weight):
    row_total = crop_tokens.shape[0]
    embedded = jnp.dot(crop_tokens, embed_weight, preferred_element_type=jnp.float32)
    first_root = jnp.sqrt(lax.optimization_barrier(jnp.mean(embedded * embedded, axis=-1, keepdims=True)) + EPSILON)
    first_unit = embedded / first_root
    normed = (first_unit * pre_gain).astype(jnp.bfloat16)
    hidden = jnp.dot(normed, up_weight, preferred_element_type=jnp.float32)
    active = jax.nn.gelu(hidden, approximate=True).astype(jnp.bfloat16)
    summed = embedded + jnp.dot(active, down_weight, preferred_element_type=jnp.float32)
    second_root = jnp.sqrt(lax.optimization_barrier(jnp.mean(summed * summed, axis=-1, keepdims=True)) + EPSILON)
    second_unit = summed / second_root
    reward = jnp.mean(lax.optimization_barrier(jnp.sum(second_unit * post_gain * head_weight, axis=-1)))
    head_slope = -(LOSS_SCALE / row_total) * head_weight * post_gain
    summed_slope = (head_slope - second_unit * lax.optimization_barrier(jnp.mean(head_slope * second_unit, axis=-1, keepdims=True))) / second_root
    active_slope = jnp.dot(summed_slope.astype(jnp.bfloat16), down_weight.T, preferred_element_type=jnp.float32)
    hidden_slope = gelu_slope(hidden, active_slope).astype(jnp.bfloat16)
    normed_slope = jnp.dot(hidden_slope, up_weight.T, preferred_element_type=jnp.float32) * pre_gain
    embed_slope = summed_slope + (normed_slope - first_unit * lax.optimization_barrier(jnp.mean(normed_slope * first_unit, axis=-1, keepdims=True))) / first_root
    token_slope = jnp.dot(embed_slope.astype(jnp.bfloat16), embed_weight.T, preferred_element_type=jnp.float32)
    return (reward, token_slope)

def clip_pass(operands, weights):
    stream, queries, keys, values, clip_length, mod_shift, mod_scale, noisy_rows, noise_step, crop_rows = operands
    out_weight, final_weight, embed_weight, pre_gain, up_weight, down_weight, post_gain, head_weight = weights
    sequence = queries.shape[0]
    per_group = HEADS // KV_HEADS
    is_live = jnp.arange(sequence, dtype=jnp.int32) < clip_length
    query_heads = jnp.transpose(queries.reshape(sequence, KV_HEADS, per_group, HEAD), (1, 0, 2, 3))
    key_heads = jnp.transpose(keys.reshape(sequence, KV_HEADS, HEAD), (1, 0, 2))
    value_heads = jnp.transpose(values.reshape(sequence, KV_HEADS, HEAD), (1, 0, 2))

    def scores_of(query_block, key_block):
        scores = jnp.einsum('tgd,sd->gts', query_block.astype(jnp.float32), key_block.astype(jnp.float32)) / math.sqrt(HEAD)
        return jnp.where(is_live[None, None, :], scores, MASKED)

    def attend(blocks):
        query_block, key_block, value_block = blocks
        scores = scores_of(query_block, key_block)
        highest = lax.optimization_barrier(jnp.max(scores, axis=-1, keepdims=True))
        weights_rows = jnp.exp(scores - highest)
        denominator = lax.optimization_barrier(jnp.sum(weights_rows, axis=-1, keepdims=True))
        blended = jnp.einsum('gts,sd->gtd', rounded(weights_rows), value_block.astype(jnp.float32)) / denominator
        return (blended, (highest + jnp.log(denominator))[..., 0])
    blended, log_total = lax.map(attend, (query_heads, key_heads, value_heads))
    attended = jnp.transpose(blended, (2, 0, 1, 3)).reshape(sequence, HEADS * HEAD).astype(jnp.bfloat16)
    residual = stream.astype(jnp.float32) + jnp.dot(attended, out_weight, preferred_element_type=jnp.float32)
    centred = residual - lax.optimization_barrier(jnp.mean(residual, axis=-1, keepdims=True))
    inverse = lax.rsqrt(lax.optimization_barrier(jnp.mean(centred * centred, axis=-1, keepdims=True)) + EPSILON)
    unit_rows = centred * inverse
    gain_rows = 1.0 + mod_scale
    modulated = (unit_rows * gain_rows + mod_shift).astype(jnp.bfloat16)
    predicted = jnp.dot(modulated, final_weight, preferred_element_type=jnp.float32)
    signal_root, noise_root = plan(noise_step)
    denoised = ((noisy_rows.astype(jnp.float32) - noise_root * predicted) / signal_root).astype(jnp.bfloat16)
    crop_tokens = denoised[crop_rows]
    reward, token_slope = reward_model(crop_tokens, embed_weight, pre_gain, up_weight, down_weight, post_gain, head_weight)
    latent_slope = jnp.zeros((sequence, PATCH), jnp.float32).at[crop_rows].add(token_slope)
    noise_slope = (-(noise_root / signal_root) * latent_slope).astype(jnp.bfloat16)
    modulated_slope = jnp.dot(noise_slope, final_weight.T, preferred_element_type=jnp.float32) * gain_rows
    residual_slope = (modulated_slope - lax.optimization_barrier(jnp.mean(modulated_slope, axis=-1, keepdims=True)) - unit_rows * lax.optimization_barrier(jnp.mean(modulated_slope * unit_rows, axis=-1, keepdims=True))) * inverse
    grad_stream = residual_slope.astype(jnp.bfloat16)
    attended_slope = jnp.dot(grad_stream, out_weight.T, preferred_element_type=jnp.float32).astype(jnp.bfloat16)
    slope_heads = jnp.transpose(attended_slope.reshape(sequence, KV_HEADS, per_group, HEAD), (1, 0, 2, 3))
    attended_heads = jnp.transpose(attended.reshape(sequence, KV_HEADS, per_group, HEAD), (1, 0, 2, 3))

    def query_grad(blocks):
        query_block, key_block, value_block, slope_block, attended_block, log_block = blocks
        scores = scores_of(query_block, key_block)
        weights_rows = jnp.exp(scores - log_block[..., None])
        row_delta = lax.optimization_barrier(jnp.sum(slope_block.astype(jnp.float32) * attended_block.astype(jnp.float32), axis=-1)).T
        slopes = jnp.einsum('tgd,sd->gts', slope_block.astype(jnp.float32), value_block.astype(jnp.float32))
        score_slope = rounded(weights_rows * (slopes - row_delta[..., None]))
        return jnp.einsum('gts,sd->gtd', score_slope, key_block.astype(jnp.float32)) / math.sqrt(HEAD)
    gradients = lax.map(query_grad, (query_heads, key_heads, value_heads, slope_heads, attended_heads, log_total))
    grad_queries = jnp.transpose(gradients, (2, 0, 1, 3)).reshape(sequence, HEADS * HEAD).astype(jnp.bfloat16)
    return (reward, grad_stream, grad_queries)

def reference(stream, queries, keys, values, clip_lengths, mod_shift, mod_scale, out_weight, final_weight, noisy_latents, timestep, crop_map, embed_weight, pre_gain, up_weight, down_weight, post_gain, head_weight):
    weights = (out_weight, final_weight, embed_weight, pre_gain, up_weight, down_weight, post_gain, head_weight)
    reward, grad_stream, grad_queries = lax.map(lambda operands: clip_pass(operands, weights), (stream, queries, keys, values, clip_lengths, mod_shift, mod_scale, noisy_latents, timestep, crop_map))
    return (reward, grad_stream, grad_queries)
```

```python
import functools
import math

import jax
import jax.numpy as jnp
from jax import lax
from jax.experimental import pallas as pl
from jax.experimental.pallas import tpu as pltpu
from jax.sharding import PartitionSpec as P

HEADS = 16
KV_HEADS = 4
HEAD = 128
PATCH = 128


MASKED = -1e30
LOSS_SCALE = 16.0
EPSILON = 1e-06
MESH = pl.DeviceIdType.MESH
VMEM_SPEC = pl.BlockSpec(memory_space=pltpu.VMEM)


def remote(src, dst, send, recv, axis, peer):
    return pltpu.make_async_remote_copy(
        src_ref=src,
        dst_ref=dst,
        send_sem=send,
        recv_sem=recv,
        device_id={axis: peer},
        device_id_type=MESH,
    )


def greet(axis, peers):
    barrier = pltpu.get_barrier_semaphore()
    for peer in peers:
        pl.semaphore_signal(barrier, inc=1, device_id={axis: peer}, device_id_type=MESH)
    pl.semaphore_wait(barrier, len(peers))


def params(collective_id):
    return pltpu.CompilerParams(
        collective_id=collective_id, has_side_effects=True, vmem_limit_bytes=48 * 1024 * 1024
    )


def swap_start(n, src, dst, send, recv):
    me = lax.axis_index("ctx")
    copies = []
    for k in range(1, n):
        peer = lax.rem(me + k, n)
        copy = remote(src.at[peer], dst.at[me], send.at[k - 1], recv.at[k - 1], "ctx", peer)
        copy.start()
        copies.append(copy)
    return copies


def swap_kernel(n, src, dst, send, recv, local):
    me = lax.axis_index("ctx")
    greet("ctx", [lax.rem(me + k, n) for k in range(1, n)])
    copies = swap_start(n, src, dst, send, recv)
    own = pltpu.make_async_copy(src.at[me], dst.at[me], local)
    own.start()
    own.wait()
    for copy in copies:
        copy.wait()


def swap(pieces, n, collective_id):
    return pl.pallas_call(
        functools.partial(swap_kernel, n),
        out_shape=jax.ShapeDtypeStruct(pieces.shape, pieces.dtype),
        in_specs=[VMEM_SPEC],
        out_specs=VMEM_SPEC,
        scratch_shapes=[
            pltpu.SemaphoreType.DMA((n - 1,)),
            pltpu.SemaphoreType.DMA((n - 1,)),
            pltpu.SemaphoreType.DMA,
        ],
        compiler_params=params(collective_id),
    )(pieces)


def front_kernel(
    n, dp_n, src, weight, dst, full, send, recv, local, up_s, up_r, dn_s, dn_r, ac_s, ac_r
):
    me = lax.axis_index("ctx")
    mine = lax.axis_index("dp")
    n_out = dp_n // 2
    outer, inner = mine // 2, lax.rem(mine, 2)
    across = outer * 2 + 1 - inner
    above, below = lax.rem(mine + 2, dp_n), lax.rem(mine + dp_n - 2, dp_n)
    has_up, has_down = outer + 1 < n_out, outer >= 1
    width = weight.shape[1]

    def block(index):
        return full.at[:, pl.ds(pl.multiple_of(index * width, width), width)]

    barrier = pltpu.get_barrier_semaphore()
    for k in range(1, n):
        pl.semaphore_signal(
            barrier, inc=1, device_id={"ctx": lax.rem(me + k, n)}, device_id_type=MESH
        )
    for peer in (across, above, below):
        pl.semaphore_signal(barrier, inc=1, device_id={"dp": peer}, device_id_type=MESH)
    pl.semaphore_wait(barrier, n + 2)
    copies = swap_start(n, src, dst, send, recv)

    def up(source, index, step):
        return remote(source, block(index), up_s.at[step], up_r.at[step], "dp", above)

    def down(source, index, step):
        return remote(source, block(index), dn_s.at[step], dn_r.at[step], "dp", below)

    def cross(source, index, step):
        return remote(source, block(index), ac_s.at[step], ac_r.at[step], "dp", across)

    pl.when(has_up)(lambda: up(weight, mine, 0).start())
    pl.when(has_down)(lambda: down(weight, mine, 0).start())
    cross(weight, mine, 0).start()
    own = pltpu.make_async_copy(src.at[me], dst.at[me], local.at[0])
    own.start()
    own_weight = pltpu.make_async_copy(weight, block(mine), local.at[1])
    own_weight.start()
    for step in range(1, n_out):
        low, high = mine - 2 * step, mine + 2 * step

        @pl.when(outer >= step)
        def _():
            up(block(low), low, step - 1).wait_recv()
            pl.when(has_up)(lambda: up(block(low), low, step).start())
            cross(block(low), low, step).start()

        @pl.when(outer + step < n_out)
        def _():
            down(block(high), high, step - 1).wait_recv()
            pl.when(has_down)(lambda: down(block(high), high, step).start())
            cross(block(high), high, n_out + step).start()

    own.wait()
    own_weight.wait()
    for copy in copies:
        copy.wait()
    pl.when(has_up)(lambda: up(weight, mine, 0).wait_send())
    pl.when(has_down)(lambda: down(weight, mine, 0).wait_send())
    cross(weight, mine, 0).wait()
    for step in range(1, n_out):
        low, high = mine - 2 * step, mine + 2 * step

        @pl.when(outer >= step)
        def _():
            pl.when(has_up)(lambda: up(block(low), low, step).wait_send())
            cross(block(low), low, step).wait()

        @pl.when(outer + step < n_out)
        def _():
            pl.when(has_down)(lambda: down(block(high), high, step).wait_send())
            cross(block(high), high, n_out + step).wait()


def front(pieces, weight, n, dp_n, collective_id):
    dma = pltpu.SemaphoreType.DMA
    n_out = dp_n // 2
    return pl.pallas_call(
        functools.partial(front_kernel, n, dp_n),
        out_shape=(
            jax.ShapeDtypeStruct(pieces.shape, pieces.dtype),
            jax.ShapeDtypeStruct((weight.shape[0], weight.shape[1] * dp_n), weight.dtype),
        ),
        in_specs=[VMEM_SPEC] * 2,
        out_specs=(VMEM_SPEC, VMEM_SPEC),
        scratch_shapes=[dma((n - 1,)), dma((n - 1,)), dma((2,))]
        + [dma((n_out,))] * 4
        + [dma((2 * n_out,))] * 2,
        compiler_params=params(collective_id),
    )(pieces, weight)


def collect_kernel(n, src, dst, send, recv, local):
    me = lax.axis_index("ctx")
    n_out = n // 2
    outer, core = me // 2, lax.rem(me, 2)
    partner = outer * 2 + 1 - core
    peers = [lax.rem(outer + k, n_out) * 2 + core for k in range(1, n_out)]
    greet("ctx", peers + [partner])
    copies = []
    for k, peer in enumerate(peers):
        copy = remote(src, dst.at[me], send.at[k + 1], recv.at[k + 1], "ctx", peer)
        copy.start()
        copies.append(copy)
    first = remote(src, dst.at[me], send.at[0], recv.at[0], "ctx", partner)
    first.start()
    own = pltpu.make_async_copy(src, dst.at[me], local)
    own.start()
    relays = []
    for k, copy in enumerate(copies):
        copy.wait_recv()
        held = lax.rem(outer + n_out - k - 1, n_out) * 2 + core
        relay = remote(
            dst.at[held], dst.at[held], send.at[n_out + k], recv.at[n_out + k], "ctx", partner
        )
        relay.start()
        relays.append(relay)
    own.wait()
    first.wait()
    for copy in copies:
        copy.wait_send()
    for relay in relays:
        relay.wait()


def collect(piece, n, collective_id):
    return pl.pallas_call(
        functools.partial(collect_kernel, n),
        out_shape=jax.ShapeDtypeStruct((n,) + piece.shape, piece.dtype),
        in_specs=[VMEM_SPEC],
        out_specs=VMEM_SPEC,
        scratch_shapes=[
            pltpu.SemaphoreType.DMA((n,)),
            pltpu.SemaphoreType.DMA((n,)),
            pltpu.SemaphoreType.DMA,
        ],
        compiler_params=params(collective_id),
    )(piece)


def reduce_kernel(n, src, dst, near, paired, far, near_s, near_r, far_s, far_r):
    me = lax.axis_index("ctx")
    n_out = n // 2
    outer, core = me // 2, lax.rem(me, 2)
    partner = outer * 2 + 1 - core
    rows = dst.shape[0]
    chunk = 16
    owners = [lax.rem(outer + k, n_out) for k in range(n_out)]
    greet("ctx", [owner * 2 + core for owner in owners[1:]] + [partner])
    nears = {}
    for k in list(range(1, n_out)) + [0]:
        copy = remote(
            src.at[owners[k] * 2 + 1 - core],
            near.at[k],
            near_s.at[k],
            near_r.at[k],
            "ctx",
            partner,
        )
        copy.start()
        nears[k] = copy
    fars = []
    for k in range(1, n_out):
        nears[k].wait_recv()
        source = owners[k] * 2 + core

        @pl.loop(0, rows // chunk)
        def _(r):
            at = pl.ds(pl.multiple_of(r * chunk, chunk), chunk)
            total = src[source, at, :].astype(jnp.float32) + near[k, at, :].astype(jnp.float32)
            paired[k - 1, at, :] = total.astype(jnp.bfloat16)

        copy = remote(
            paired.at[k - 1], far.at[k - 1], far_s.at[k - 1], far_r.at[k - 1], "ctx", source
        )
        copy.start()
        fars.append(copy)
    nears[0].wait_recv()
    for copy in fars:
        copy.wait_recv()

    @pl.loop(0, rows // chunk)
    def _(r):
        at = pl.ds(pl.multiple_of(r * chunk, chunk), chunk)
        total = src[me, at, :].astype(jnp.float32) + near[0, at, :].astype(jnp.float32)
        for k in range(n_out - 1):
            total = total + far[k, at, :].astype(jnp.float32)
        dst[at, :] = total

    for k in range(n_out):
        nears[k].wait_send()
    for copy in fars:
        copy.wait_send()


def reduce(pieces, n, collective_id):
    shape = pieces.shape[1:]
    n_out = n // 2
    dma = pltpu.SemaphoreType.DMA
    return pl.pallas_call(
        functools.partial(reduce_kernel, n),
        out_shape=jax.ShapeDtypeStruct(shape, jnp.float32),
        in_specs=[VMEM_SPEC],
        out_specs=VMEM_SPEC,
        scratch_shapes=[
            pltpu.VMEM((n_out,) + shape, jnp.bfloat16),
            pltpu.VMEM((n_out - 1,) + shape, jnp.bfloat16),
            pltpu.VMEM((n_out - 1,) + shape, jnp.bfloat16),
            dma((n_out,)),
            dma((n_out,)),
            dma((n_out - 1,)),
            dma((n_out - 1,)),
        ],
        compiler_params=params(collective_id),
    )(pieces)


def plan(noise_step):
    phase = (noise_step.astype(jnp.float32) / 1000.0 + 0.008) / 1.008 * (math.pi / 2.0)
    signal_root = jnp.cos(phase)
    return (signal_root, jnp.sqrt(1.0 - signal_root * signal_root))


def gelu_slope(hidden, upstream):
    return jax.vjp(lambda argument: jax.nn.gelu(argument, approximate=True), hidden)[1](upstream)[0]


def matmul(subscripts, left, right):
    return jnp.einsum(subscripts, left, right, preferred_element_type=jnp.float32)


def per_device(
    n,
    dp_n,
    stream,
    queries,
    keys,
    values,
    clip_lengths,
    mod_shift,
    mod_scale,
    out_weight,
    final_weight,
    noisy_latents,
    timestep,
    crop_map,
    embed_weight,
    pre_gain,
    up_weight,
    down_weight,
    post_gain,
    head_weight,
):
    tokens = queries.shape[1]
    sequence = tokens * n
    width = stream.shape[2]
    heads = HEADS // n
    per_group = HEADS // KV_HEADS
    me = lax.axis_index("ctx")
    clip_length = clip_lengths[0]

    groups = [(c * heads) // per_group for c in range(n)]
    pieces = jnp.stack(
        [
            jnp.concatenate(
                [
                    queries[0, :, c * heads * HEAD : (c + 1) * heads * HEAD],
                    keys[0, :, groups[c] * HEAD : (groups[c] + 1) * HEAD],
                    values[0, :, groups[c] * HEAD : (groups[c] + 1) * HEAD],
                ],
                axis=-1,
            )
            for c in range(n)
        ]
    )
    swapped, weight = front(pieces, out_weight, n, dp_n, 0)
    swapped = swapped.reshape(sequence, (heads + 2) * HEAD)
    query_heads = swapped[:, : heads * HEAD].reshape(sequence, heads, HEAD)
    key_rows = swapped[:, heads * HEAD : (heads + 1) * HEAD]
    value_rows = swapped[:, (heads + 1) * HEAD :]

    is_live = jnp.arange(sequence, dtype=jnp.int32) < clip_length
    scores = matmul("thd,sd->hts", query_heads, key_rows) / math.sqrt(HEAD)
    scores = jnp.where(is_live, scores, MASKED)
    highest = jnp.max(scores, axis=-1)
    weights_rows = jnp.exp(scores - highest[..., None])
    denominator = jnp.sum(weights_rows, axis=-1)
    numerator = matmul("hts,sd->htd", weights_rows.astype(jnp.bfloat16), value_rows)
    attended_heads = (numerator / denominator[..., None]).astype(jnp.bfloat16)
    attended = jnp.transpose(attended_heads, (1, 0, 2)).reshape(sequence, heads * HEAD)
    log_total = highest + jnp.log(denominator)

    product = matmul("tr,rc->tc", attended, weight).astype(jnp.bfloat16)
    residual = stream[0].astype(jnp.float32) + reduce(product.reshape(n, tokens, width), n, 1)
    centred = residual - jnp.mean(residual, axis=-1, keepdims=True)
    inverse = lax.rsqrt(jnp.mean(centred * centred, axis=-1, keepdims=True) + EPSILON)
    unit_rows = centred * inverse
    gain_rows = 1.0 + mod_scale[0]
    modulated = (unit_rows * gain_rows + mod_shift[0]).astype(jnp.bfloat16)
    predicted = jnp.dot(modulated, final_weight, preferred_element_type=jnp.float32)
    signal_root, noise_root = plan(timestep[0])
    denoised = (
        (noisy_latents[0].astype(jnp.float32) - noise_root * predicted) / signal_root
    ).astype(jnp.bfloat16)

    final_wide = final_weight.astype(jnp.float32)
    gained = final_wide * gain_rows[:, None]
    gained_mean = jnp.mean(gained, axis=0)
    along_unit = predicted - jnp.sum(final_wide * mod_shift[0][:, None], axis=0)
    bundle = jnp.concatenate(
        [
            denoised,
            along_unit.astype(jnp.bfloat16),
            jnp.broadcast_to(inverse, (tokens, PATCH)).astype(jnp.bfloat16),
        ],
        axis=-1,
    )
    bundles = collect(bundle, n, 2).reshape(sequence, 3 * PATCH)
    gathered = bundles[:, :PATCH]
    unit_full = lax.all_gather(unit_rows.astype(jnp.bfloat16), "ctx", axis=0, tiled=True)
    unit_out = matmul("tc,rc->tr", unit_full, weight)
    gained_out = matmul("rc,cp->rp", weight, gained.astype(jnp.bfloat16)).astype(jnp.bfloat16)
    weight_sum = jnp.sum(weight.astype(jnp.float32), axis=-1)

    crop_rows = crop_map[0]
    crop_tokens = jnp.take(gathered, crop_rows, axis=0)
    embedded = jnp.dot(crop_tokens, embed_weight, preferred_element_type=jnp.float32)
    first_root = jnp.sqrt(jnp.mean(embedded * embedded, axis=-1, keepdims=True) + EPSILON)
    first_unit = embedded / first_root
    normed = (first_unit * pre_gain).astype(jnp.bfloat16)
    hidden = jnp.dot(normed, up_weight, preferred_element_type=jnp.float32)
    active = jax.nn.gelu(hidden, approximate=True).astype(jnp.bfloat16)
    row_total, reward_width = embedded.shape
    rows = row_total // n

    def own_rows(whole):
        return lax.dynamic_slice_in_dim(whole, me * rows, rows, 0)

    head_slope = -(LOSS_SCALE / row_total) * head_weight * post_gain
    down_part = jnp.dot(active, down_weight, preferred_element_type=jnp.float32)
    summed = own_rows(embedded) + reduce(
        down_part.astype(jnp.bfloat16).reshape(n, rows, reward_width), n, 3
    )
    second_root = jnp.sqrt(jnp.mean(summed * summed, axis=-1, keepdims=True) + EPSILON)
    second_unit = summed / second_root
    row_rewards = jnp.sum(second_unit * post_gain * head_weight, axis=-1, keepdims=True)
    summed_slope = (
        head_slope - second_unit * jnp.mean(head_slope * second_unit, axis=-1, keepdims=True)
    ) / second_root
    summed_slopes = collect(summed_slope.astype(jnp.bfloat16), n, 4).reshape(
        row_total, reward_width
    )
    active_slope = matmul("rw,hw->rh", summed_slopes, down_weight)
    hidden_slope = gelu_slope(hidden, active_slope).astype(jnp.bfloat16)
    up_part = matmul("rh,wh->rw", hidden_slope, up_weight)
    normed_slope = (
        reduce(up_part.astype(jnp.bfloat16).reshape(n, rows, reward_width), n, 5) * pre_gain
    )
    own_unit = own_rows(first_unit)
    embed_slope = (
        summed_slope
        + (normed_slope - own_unit * jnp.mean(normed_slope * own_unit, axis=-1, keepdims=True))
        / own_rows(first_root)
    )
    token_slope = matmul("rw,pw->rp", embed_slope.astype(jnp.bfloat16), embed_weight)
    token_slopes = collect(
        jnp.concatenate([token_slope, jnp.broadcast_to(row_rewards, (rows, PATCH))], axis=-1), n, 6
    ).reshape(row_total, 2 * PATCH)
    reward = jnp.mean(token_slopes[:, PATCH])
    latent_full = (
        jnp.zeros((sequence, PATCH), jnp.float32).at[crop_rows].add(token_slopes[:, :PATCH])
    )
    noise_slopes = (-(noise_root / signal_root) * latent_full).astype(jnp.bfloat16)
    noise_slope = lax.dynamic_slice_in_dim(noise_slopes, me * tokens, tokens, 0)
    modulated_slope = matmul("tp,dp->td", noise_slope, final_weight) * gain_rows
    residual_slope = (
        modulated_slope
        - jnp.mean(modulated_slope, axis=-1, keepdims=True)
        - unit_rows * jnp.mean(modulated_slope * unit_rows, axis=-1, keepdims=True)
    ) * inverse
    grad_stream = residual_slope.astype(jnp.bfloat16)

    noise_wide = noise_slopes.astype(jnp.float32)
    slope_mean = jnp.sum(noise_wide * gained_mean, axis=-1, keepdims=True)
    slope_along = (
        jnp.sum(
            noise_wide * bundles[:, PATCH : 2 * PATCH].astype(jnp.float32), axis=-1, keepdims=True
        )
        / width
    )
    attended_slope = (
        (
            matmul("tp,rp->tr", noise_slopes, gained_out)
            - slope_mean * weight_sum
            - slope_along * unit_out
        )
        * bundles[:, 2 * PATCH : 2 * PATCH + 1].astype(jnp.float32)
    ).astype(jnp.bfloat16)
    slope_heads = attended_slope.reshape(sequence, heads, HEAD)
    row_delta = jnp.sum(
        jnp.transpose(slope_heads, (1, 0, 2)).astype(jnp.float32)
        * attended_heads.astype(jnp.float32),
        axis=-1,
    )
    back_scores = matmul("thd,sd->hts", query_heads, key_rows) / math.sqrt(HEAD)
    back_scores = jnp.where(is_live, back_scores, MASKED)
    back_weights = jnp.exp(back_scores - log_total[..., None])
    slopes = matmul("thd,sd->hts", slope_heads, value_rows)
    score_slope = (back_weights * (slopes - row_delta[..., None])).astype(jnp.bfloat16)
    query_slope = matmul("hts,sd->htd", score_slope, key_rows) / math.sqrt(HEAD)
    by_head = (
        jnp.transpose(query_slope, (1, 0, 2))
        .reshape(n, tokens, heads * HEAD)
        .astype(jnp.bfloat16)
    )
    grad_queries = jnp.transpose(swap(by_head, n, 7), (1, 0, 2)).reshape(tokens, HEADS * HEAD)
    return (jnp.reshape(reward, (1,)), grad_stream[None], grad_queries[None])


def solution(mesh):
    return jax.shard_map(
        functools.partial(per_device, mesh.shape["ctx"], mesh.shape["dp"]),
        mesh=mesh,
        in_specs=(
            P("dp", "ctx", None),
            P("dp", "ctx", None),
            P("dp", "ctx", None),
            P("dp", "ctx", None),
            P("dp"),
            P("dp", None),
            P("dp", None),
            P("ctx", "dp"),
            P(),
            P("dp", "ctx", None),
            P("dp"),
            P("dp", None),
            P(),
            P(),
            P(None, "ctx"),
            P("ctx", None),
            P(),
            P(),
        ),
        out_specs=(P("dp"), P("dp", "ctx", None), P("dp", "ctx", None)),
        check_vma=False,
    )
```

```python
import functools
import math

import jax
import jax.numpy as jnp
from jax import lax
from jax.experimental import pallas as pl
from jax.experimental.pallas import tpu as pltpu
from jax.sharding import PartitionSpec as P

HEADS = 16
KV_HEADS = 4
HEAD = 128
PATCH = 128


MASKED = -1e30
LOSS_SCALE = 16.0
EPSILON = 1e-06
MESH = pl.DeviceIdType.MESH
VMEM_SPEC = pl.BlockSpec(memory_space=pltpu.VMEM)


def remote(src, dst, send, recv, axis, peer):
    return pltpu.make_async_remote_copy(
        src_ref=src,
        dst_ref=dst,
        send_sem=send,
        recv_sem=recv,
        device_id={axis: peer},
        device_id_type=MESH,
    )


def greet(axis, peers):
    barrier = pltpu.get_barrier_semaphore()
    for peer in peers:
        pl.semaphore_signal(barrier, inc=1, device_id={axis: peer}, device_id_type=MESH)
    pl.semaphore_wait(barrier, len(peers))


def params(collective_id):
    return pltpu.CompilerParams(
        collective_id=collective_id, has_side_effects=True, vmem_limit_bytes=48 * 1024 * 1024
    )


def swap_start(n, src, dst, send, recv):
    me = lax.axis_index("ctx")
    copies = []
    for k in range(1, n):
        peer = lax.rem(me + k, n)
        copy = remote(src.at[peer], dst.at[me], send.at[k - 1], recv.at[k - 1], "ctx", peer)
        copy.start()
        copies.append(copy)
    return copies


def swap_kernel(n, src, dst, send, recv, local):
    me = lax.axis_index("ctx")
    greet("ctx", [lax.rem(me + k, n) for k in range(1, n)])
    copies = swap_start(n, src, dst, send, recv)
    own = pltpu.make_async_copy(src.at[me], dst.at[me], local)
    own.start()
    own.wait()
    for copy in copies:
        copy.wait()


def swap(pieces, n, collective_id):
    return pl.pallas_call(
        functools.partial(swap_kernel, n),
        out_shape=jax.ShapeDtypeStruct(pieces.shape, pieces.dtype),
        in_specs=[VMEM_SPEC],
        out_specs=VMEM_SPEC,
        scratch_shapes=[
            pltpu.SemaphoreType.DMA((n - 1,)),
            pltpu.SemaphoreType.DMA((n - 1,)),
            pltpu.SemaphoreType.DMA,
        ],
        compiler_params=params(collective_id),
    )(pieces)


def front_kernel(
    n,
    dp_n,
    heads,
    src,
    weight,
    live,
    dst,
    full,
    attended,
    log_total,
    total,
    product,
    near,
    paired,
    far,
    send,
    recv,
    local,
    up_s,
    dn_s,
    z_r,
    x_s,
    x_r,
    near_s,
    near_r,
    far_s,
    far_r,
):
    me = lax.axis_index("ctx")
    mine = lax.axis_index("dp")
    n_out = dp_n // 2
    outer, inner = mine // 2, lax.rem(mine, 2)
    across = outer * 2 + 1 - inner
    above, below = lax.rem(mine + 2, dp_n), lax.rem(mine + dp_n - 2, dp_n)
    has_up, has_down = outer + 1 < n_out, outer >= 1
    width = weight.shape[1]
    tokens = src.shape[1]
    n_ctx = n // 2
    ctx_out, core = me // 2, lax.rem(me, 2)
    partner = ctx_out * 2 + 1 - core
    owners = [lax.rem(ctx_out + k, n_ctx) * 2 for k in range(n_ctx)]

    def columns(index):
        return pl.ds(pl.multiple_of(index * width, width), width)

    def block(index):
        return full.at[:, columns(index)]

    barrier = pltpu.get_barrier_semaphore()
    for k in range(1, n):
        pl.semaphore_signal(
            barrier, inc=1, device_id={"ctx": lax.rem(me + k, n)}, device_id_type=MESH
        )
    for peer in (across, above, below):
        pl.semaphore_signal(barrier, inc=1, device_id={"dp": peer}, device_id_type=MESH)
    pl.semaphore_wait(barrier, n + 2)

    side = jnp.minimum(outer, n_out - 1 - outer)
    origins = [outer]
    for j in range(1, n_out):
        paired_step = (j + 1) // 2
        near_origin = outer - paired_step if j % 2 == 1 else outer + paired_step
        far_origin = jnp.where(outer > n_out - 1 - outer, outer - (j - side), outer + (j - side))
        origins.append(jnp.where(j <= 2 * side, near_origin, far_origin))

    def up(j):
        at = origins[j]
        source = weight if j == 0 else block(at * 2 + inner)
        return remote(source, block(at * 2 + inner), up_s.at[at], z_r.at[at], "dp", above)

    def down(j):
        at = origins[j]
        source = weight if j == 0 else block(at * 2 + inner)
        return remote(source, block(at * 2 + inner), dn_s.at[at], z_r.at[at], "dp", below)

    def cross(j):
        at = origins[j]
        source = weight if j == 0 else block(at * 2 + inner)
        return remote(source, block(at * 2 + inner), x_s.at[at], x_r.at[at], "dp", across)

    def goes_up(j):
        return has_up if j == 0 else jnp.logical_and(has_up, origins[j] < outer)

    def goes_down(j):
        return has_down if j == 0 else jnp.logical_and(has_down, origins[j] > outer)

    own_weight = pltpu.make_async_copy(weight, block(mine), local.at[1])

    def acquire(kind, j):
        if kind == "x":
            cross(j).wait_recv()
            return origins[j] * 2 + 1 - inner
        if j:
            up(j).wait_recv()
        pl.when(goes_up(j))(lambda: up(j).start())
        pl.when(goes_down(j))(lambda: down(j).start())
        cross(j).start()
        if j == 0:
            own_weight.start()
            own_weight.wait()
        return origins[j] * 2 + inner

    copies = swap_start(n, src, dst, send, recv)
    own = pltpu.make_async_copy(src.at[me], dst.at[me], local.at[0])
    own.start()
    slots = [("z", 0)]
    for j in range(1, n_out):
        slots += [("z", j), ("x", j - 1)]
    slots.append(("x", n_out - 1))
    positions = [acquire(*slots[0])]
    own.wait()
    for copy in copies:
        copy.wait()

    sequence = n * tokens
    keys = dst[:, :, heads * HEAD : (heads + 1) * HEAD].reshape(sequence, HEAD)
    values = dst[:, :, (heads + 1) * HEAD :].reshape(sequence, HEAD)
    is_live = live[...] > 0.5
    group = min(n, 4)
    pieces = [(h, r) for h in range(heads) for r in range(0, n, group)]
    for step, (h, r) in enumerate(pieces):
        at = slice(r * tokens, (r + group) * tokens)
        queries = dst[r : r + group, :, h * HEAD : (h + 1) * HEAD].reshape(group * tokens, HEAD)
        scores = lax.dot_general(
            queries, keys, (((1,), (1,)), ((), ())), preferred_element_type=jnp.float32
        ) / math.sqrt(HEAD)
        scores = jnp.where(is_live, scores, MASKED)
        highest = jnp.max(scores, axis=-1, keepdims=True)
        weights_rows = jnp.exp(scores - highest)
        denominator = jnp.sum(weights_rows, axis=-1, keepdims=True)
        numerator = jnp.dot(
            weights_rows.astype(jnp.bfloat16), values, preferred_element_type=jnp.float32
        )
        attended[at, h * HEAD : (h + 1) * HEAD] = (numerator / denominator).astype(jnp.bfloat16)
        log_total[at, h : h + 1] = highest + jnp.log(denominator)
        if step == len(pieces) // 2 - 1:
            positions.append(acquire(*slots[1]))

    def near_copy(t, k):
        source = product.at[t, owners[k] + 1 - core]
        return remote(source, near.at[t, k], near_s.at[t, k], near_r.at[t, k], "ctx", partner)

    def far_copy(t, k):
        return remote(
            paired.at[t, k - 1],
            far.at[t, k - 1],
            far_s.at[t, k - 1],
            far_r.at[t, k - 1],
            "ctx",
            owners[k] + core,
        )

    def pair(t):
        for k in range(1, n_ctx):
            near_copy(t, k).wait_recv()
            paired[t, k - 1] = (
                product[t, owners[k] + core].astype(jnp.float32) + near[t, k].astype(jnp.float32)
            ).astype(jnp.bfloat16)
            far_copy(t, k).start()

    for t, slot in enumerate(slots):
        if t >= len(positions):
            positions.append(acquire(*slot))
        part = jnp.dot(
            attended[...], full[:, columns(positions[t])], preferred_element_type=jnp.float32
        )
        product[t] = part.astype(jnp.bfloat16).reshape(n, tokens, width)
        for k in list(range(1, n_ctx)) + [0]:
            near_copy(t, k).start()
        if t:
            pair(t - 1)
    pair(len(slots) - 1)
    for t in range(len(slots)):
        near_copy(t, 0).wait_recv()
        whole = product[t, me].astype(jnp.float32) + near[t, 0].astype(jnp.float32)
        for k in range(1, n_ctx):
            far_copy(t, k).wait_recv()
            whole = whole + far[t, k - 1].astype(jnp.float32)
        total[:, columns(positions[t])] = whole

    for j in range(n_out):
        pl.when(goes_up(j))(lambda: up(j).wait_send())
        pl.when(goes_down(j))(lambda: down(j).wait_send())
        cross(j).wait_send()
    for t in range(len(slots)):
        for k in range(n_ctx):
            near_copy(t, k).wait_send()
        for k in range(1, n_ctx):
            far_copy(t, k).wait_send()


def front(pieces, weight, live, n, dp_n, heads, collective_id):
    dma = pltpu.SemaphoreType.DMA
    n_out, n_ctx = dp_n // 2, n // 2
    tokens = pieces.shape[1]
    rows, width = weight.shape
    part = (tokens, width)
    half = jnp.bfloat16
    return pl.pallas_call(
        functools.partial(front_kernel, n, dp_n, heads),
        out_shape=(
            jax.ShapeDtypeStruct(pieces.shape, pieces.dtype),
            jax.ShapeDtypeStruct((rows, width * dp_n), weight.dtype),
            jax.ShapeDtypeStruct((n * tokens, heads * HEAD), half),
            jax.ShapeDtypeStruct((n * tokens, heads), jnp.float32),
            jax.ShapeDtypeStruct((tokens, width * dp_n), jnp.float32),
        ),
        in_specs=[VMEM_SPEC] * 3,
        out_specs=(VMEM_SPEC,) * 5,
        scratch_shapes=[
            pltpu.VMEM((dp_n, n) + part, half),
            pltpu.VMEM((dp_n, n_ctx) + part, half),
            pltpu.VMEM((dp_n, n_ctx - 1) + part, half),
            pltpu.VMEM((dp_n, n_ctx - 1) + part, half),
            dma((n - 1,)),
            dma((n - 1,)),
            dma((2,)),
        ]
        + [dma((n_out,))] * 5
        + [dma((dp_n, n_ctx))] * 2
        + [dma((dp_n, n_ctx - 1))] * 2,
        compiler_params=params(collective_id),
    )(pieces, weight, live)


def collect_kernel(n, src, dst, send, recv, local):
    me = lax.axis_index("ctx")
    n_out = n // 2
    outer, core = me // 2, lax.rem(me, 2)
    partner = outer * 2 + 1 - core
    peers = [lax.rem(outer + k, n_out) * 2 + core for k in range(1, n_out)]
    greet("ctx", peers + [partner])
    copies = []
    for k, peer in enumerate(peers):
        copy = remote(src, dst.at[me], send.at[k + 1], recv.at[k + 1], "ctx", peer)
        copy.start()
        copies.append(copy)
    first = remote(src, dst.at[me], send.at[0], recv.at[0], "ctx", partner)
    first.start()
    own = pltpu.make_async_copy(src, dst.at[me], local)
    own.start()
    relays = []
    for k, copy in enumerate(copies):
        copy.wait_recv()
        held = lax.rem(outer + n_out - k - 1, n_out) * 2 + core
        relay = remote(
            dst.at[held], dst.at[held], send.at[n_out + k], recv.at[n_out + k], "ctx", partner
        )
        relay.start()
        relays.append(relay)
    own.wait()
    first.wait()
    for copy in copies:
        copy.wait_send()
    for relay in relays:
        relay.wait()


def collect(piece, n, collective_id):
    return pl.pallas_call(
        functools.partial(collect_kernel, n),
        out_shape=jax.ShapeDtypeStruct((n,) + piece.shape, piece.dtype),
        in_specs=[VMEM_SPEC],
        out_specs=VMEM_SPEC,
        scratch_shapes=[
            pltpu.SemaphoreType.DMA((n,)),
            pltpu.SemaphoreType.DMA((n,)),
            pltpu.SemaphoreType.DMA,
        ],
        compiler_params=params(collective_id),
    )(piece)


def reduce_kernel(n, src, dst, near, paired, far, near_s, near_r, far_s, far_r):
    me = lax.axis_index("ctx")
    n_out = n // 2
    outer, core = me // 2, lax.rem(me, 2)
    partner = outer * 2 + 1 - core
    rows = dst.shape[0]
    chunk = 16
    owners = [lax.rem(outer + k, n_out) for k in range(n_out)]
    greet("ctx", [owner * 2 + core for owner in owners[1:]] + [partner])
    nears = {}
    for k in list(range(1, n_out)) + [0]:
        copy = remote(
            src.at[owners[k] * 2 + 1 - core],
            near.at[k],
            near_s.at[k],
            near_r.at[k],
            "ctx",
            partner,
        )
        copy.start()
        nears[k] = copy
    fars = []
    for k in range(1, n_out):
        nears[k].wait_recv()
        source = owners[k] * 2 + core

        @pl.loop(0, rows // chunk)
        def _(r):
            at = pl.ds(pl.multiple_of(r * chunk, chunk), chunk)
            total = src[source, at, :].astype(jnp.float32) + near[k, at, :].astype(jnp.float32)
            paired[k - 1, at, :] = total.astype(jnp.bfloat16)

        copy = remote(
            paired.at[k - 1], far.at[k - 1], far_s.at[k - 1], far_r.at[k - 1], "ctx", source
        )
        copy.start()
        fars.append(copy)
    nears[0].wait_recv()
    for copy in fars:
        copy.wait_recv()

    @pl.loop(0, rows // chunk)
    def _(r):
        at = pl.ds(pl.multiple_of(r * chunk, chunk), chunk)
        total = src[me, at, :].astype(jnp.float32) + near[0, at, :].astype(jnp.float32)
        for k in range(n_out - 1):
            total = total + far[k, at, :].astype(jnp.float32)
        dst[at, :] = total

    for k in range(n_out):
        nears[k].wait_send()
    for copy in fars:
        copy.wait_send()


def reduce(pieces, n, collective_id):
    shape = pieces.shape[1:]
    n_out = n // 2
    dma = pltpu.SemaphoreType.DMA
    return pl.pallas_call(
        functools.partial(reduce_kernel, n),
        out_shape=jax.ShapeDtypeStruct(shape, jnp.float32),
        in_specs=[VMEM_SPEC],
        out_specs=VMEM_SPEC,
        scratch_shapes=[
            pltpu.VMEM((n_out,) + shape, jnp.bfloat16),
            pltpu.VMEM((n_out - 1,) + shape, jnp.bfloat16),
            pltpu.VMEM((n_out - 1,) + shape, jnp.bfloat16),
            dma((n_out,)),
            dma((n_out,)),
            dma((n_out - 1,)),
            dma((n_out - 1,)),
        ],
        compiler_params=params(collective_id),
    )(pieces)


def plan(noise_step):
    phase = (noise_step.astype(jnp.float32) / 1000.0 + 0.008) / 1.008 * (math.pi / 2.0)
    signal_root = jnp.cos(phase)
    return (signal_root, jnp.sqrt(1.0 - signal_root * signal_root))


def gelu_slope(hidden, upstream):
    return jax.vjp(lambda argument: jax.nn.gelu(argument, approximate=True), hidden)[1](upstream)[0]


def matmul(subscripts, left, right):
    return jnp.einsum(subscripts, left, right, preferred_element_type=jnp.float32)


def per_device(
    n,
    dp_n,
    stream,
    queries,
    keys,
    values,
    clip_lengths,
    mod_shift,
    mod_scale,
    out_weight,
    final_weight,
    noisy_latents,
    timestep,
    crop_map,
    embed_weight,
    pre_gain,
    up_weight,
    down_weight,
    post_gain,
    head_weight,
):
    tokens = queries.shape[1]
    sequence = tokens * n
    width = stream.shape[2]
    heads = HEADS // n
    per_group = HEADS // KV_HEADS
    me = lax.axis_index("ctx")
    clip_length = clip_lengths[0]

    groups = [(c * heads) // per_group for c in range(n)]
    pieces = jnp.stack(
        [
            jnp.concatenate(
                [
                    queries[0, :, c * heads * HEAD : (c + 1) * heads * HEAD],
                    keys[0, :, groups[c] * HEAD : (groups[c] + 1) * HEAD],
                    values[0, :, groups[c] * HEAD : (groups[c] + 1) * HEAD],
                ],
                axis=-1,
            )
            for c in range(n)
        ]
    )
    is_live = jnp.arange(sequence, dtype=jnp.int32) < clip_length
    swapped, weight, attended, log_total, product = front(
        pieces, out_weight, is_live.astype(jnp.float32)[None], n, dp_n, heads, 0
    )
    swapped = swapped.reshape(sequence, (heads + 2) * HEAD)
    query_heads = swapped[:, : heads * HEAD].reshape(sequence, heads, HEAD)
    key_rows = swapped[:, heads * HEAD : (heads + 1) * HEAD]
    value_rows = swapped[:, (heads + 1) * HEAD :]

    residual = stream[0].astype(jnp.float32) + product
    centred = residual - jnp.mean(residual, axis=-1, keepdims=True)
    inverse = lax.rsqrt(jnp.mean(centred * centred, axis=-1, keepdims=True) + EPSILON)
    unit_rows = centred * inverse
    gain_rows = 1.0 + mod_scale[0]
    modulated = (unit_rows * gain_rows + mod_shift[0]).astype(jnp.bfloat16)
    predicted = jnp.dot(modulated, final_weight, preferred_element_type=jnp.float32)
    signal_root, noise_root = plan(timestep[0])
    denoised = (
        (noisy_latents[0].astype(jnp.float32) - noise_root * predicted) / signal_root
    ).astype(jnp.bfloat16)

    final_wide = final_weight.astype(jnp.float32)
    gained = final_wide * gain_rows[:, None]
    gained_mean = jnp.mean(gained, axis=0)
    along_unit = predicted - jnp.sum(final_wide * mod_shift[0][:, None], axis=0)
    bundle = jnp.concatenate(
        [
            denoised,
            along_unit.astype(jnp.bfloat16),
            jnp.broadcast_to(inverse, (tokens, PATCH)).astype(jnp.bfloat16),
        ],
        axis=-1,
    )
    bundles = collect(bundle, n, 2).reshape(sequence, 3 * PATCH)
    gathered = bundles[:, :PATCH]
    unit_full = collect(unit_rows.astype(jnp.bfloat16), n, 1).reshape(sequence, width)
    unit_out = matmul("tc,rc->tr", unit_full, weight)
    gained_out = matmul("rc,cp->rp", weight, gained.astype(jnp.bfloat16)).astype(jnp.bfloat16)
    weight_sum = jnp.sum(weight.astype(jnp.float32), axis=-1)

    crop_rows = crop_map[0]
    crop_tokens = jnp.take(gathered, crop_rows, axis=0)
    embedded = jnp.dot(crop_tokens, embed_weight, preferred_element_type=jnp.float32)
    first_root = jnp.sqrt(jnp.mean(embedded * embedded, axis=-1, keepdims=True) + EPSILON)
    first_unit = embedded / first_root
    normed = (first_unit * pre_gain).astype(jnp.bfloat16)
    hidden = jnp.dot(normed, up_weight, preferred_element_type=jnp.float32)
    active = jax.nn.gelu(hidden, approximate=True).astype(jnp.bfloat16)
    row_total, reward_width = embedded.shape
    rows = row_total // n

    def own_rows(whole):
        return lax.dynamic_slice_in_dim(whole, me * rows, rows, 0)

    head_slope = -(LOSS_SCALE / row_total) * head_weight * post_gain
    down_part = jnp.dot(active, down_weight, preferred_element_type=jnp.float32)
    summed = own_rows(embedded) + reduce(
        down_part.astype(jnp.bfloat16).reshape(n, rows, reward_width), n, 3
    )
    second_root = jnp.sqrt(jnp.mean(summed * summed, axis=-1, keepdims=True) + EPSILON)
    second_unit = summed / second_root
    row_rewards = jnp.sum(second_unit * post_gain * head_weight, axis=-1, keepdims=True)
    summed_slope = (
        head_slope - second_unit * jnp.mean(head_slope * second_unit, axis=-1, keepdims=True)
    ) / second_root
    summed_slopes = collect(summed_slope.astype(jnp.bfloat16), n, 4).reshape(
        row_total, reward_width
    )
    active_slope = matmul("rw,hw->rh", summed_slopes, down_weight)
    hidden_slope = gelu_slope(hidden, active_slope).astype(jnp.bfloat16)
    up_part = matmul("rh,wh->rw", hidden_slope, up_weight)
    normed_slope = (
        reduce(up_part.astype(jnp.bfloat16).reshape(n, rows, reward_width), n, 5) * pre_gain
    )
    own_unit = own_rows(first_unit)
    embed_slope = (
        summed_slope
        + (normed_slope - own_unit * jnp.mean(normed_slope * own_unit, axis=-1, keepdims=True))
        / own_rows(first_root)
    )
    token_slope = matmul("rw,pw->rp", embed_slope.astype(jnp.bfloat16), embed_weight)
    token_slopes = collect(
        jnp.concatenate([token_slope, jnp.broadcast_to(row_rewards, (rows, PATCH))], axis=-1), n, 6
    ).reshape(row_total, 2 * PATCH)
    reward = jnp.mean(token_slopes[:, PATCH])
    latent_full = (
        jnp.zeros((sequence, PATCH), jnp.float32).at[crop_rows].add(token_slopes[:, :PATCH])
    )
    noise_slopes = (-(noise_root / signal_root) * latent_full).astype(jnp.bfloat16)
    noise_slope = lax.dynamic_slice_in_dim(noise_slopes, me * tokens, tokens, 0)
    modulated_slope = matmul("tp,dp->td", noise_slope, final_weight) * gain_rows
    residual_slope = (
        modulated_slope
        - jnp.mean(modulated_slope, axis=-1, keepdims=True)
        - unit_rows * jnp.mean(modulated_slope * unit_rows, axis=-1, keepdims=True)
    ) * inverse
    grad_stream = residual_slope.astype(jnp.bfloat16)

    noise_wide = noise_slopes.astype(jnp.float32)
    slope_mean = jnp.sum(noise_wide * gained_mean, axis=-1, keepdims=True)
    slope_along = (
        jnp.sum(
            noise_wide * bundles[:, PATCH : 2 * PATCH].astype(jnp.float32), axis=-1, keepdims=True
        )
        / width
    )
    attended_slope = (
        (
            matmul("tp,rp->tr", noise_slopes, gained_out)
            - slope_mean * weight_sum
            - slope_along * unit_out
        )
        * bundles[:, 2 * PATCH : 2 * PATCH + 1].astype(jnp.float32)
    ).astype(jnp.bfloat16)
    slope_heads = attended_slope.reshape(sequence, heads, HEAD)
    row_delta = jnp.sum(
        slope_heads.astype(jnp.float32)
        * attended.reshape(sequence, heads, HEAD).astype(jnp.float32),
        axis=-1,
    ).T
    back_scores = matmul("thd,sd->hts", query_heads, key_rows) / math.sqrt(HEAD)
    back_scores = jnp.where(is_live, back_scores, MASKED)
    back_weights = jnp.exp(back_scores - log_total.T[..., None])
    slopes = matmul("thd,sd->hts", slope_heads, value_rows)
    score_slope = (back_weights * (slopes - row_delta[..., None])).astype(jnp.bfloat16)
    query_slope = matmul("hts,sd->htd", score_slope, key_rows) / math.sqrt(HEAD)
    by_head = (
        jnp.transpose(query_slope, (1, 0, 2))
        .reshape(n, tokens, heads * HEAD)
        .astype(jnp.bfloat16)
    )
    grad_queries = jnp.transpose(swap(by_head, n, 7), (1, 0, 2)).reshape(tokens, HEADS * HEAD)
    return (jnp.reshape(reward, (1,)), grad_stream[None], grad_queries[None])


def solution(mesh):
    return jax.shard_map(
        functools.partial(per_device, mesh.shape["ctx"], mesh.shape["dp"]),
        mesh=mesh,
        in_specs=(
            P("dp", "ctx", None),
            P("dp", "ctx", None),
            P("dp", "ctx", None),
            P("dp", "ctx", None),
            P("dp"),
            P("dp", None),
            P("dp", None),
            P("ctx", "dp"),
            P(),
            P("dp", "ctx", None),
            P("dp"),
            P("dp", None),
            P(),
            P(),
            P(None, "ctx"),
            P("ctx", None),
            P(),
            P(),
        ),
        out_specs=(P("dp"), P("dp", "ctx", None), P("dp", "ctx", None)),
        check_vma=False,
    )
```

```python
import functools
import math

import jax
import jax.numpy as jnp
from jax import lax
from jax.experimental import pallas as pl
from jax.experimental.pallas import tpu as pltpu
from jax.sharding import PartitionSpec as P

HEADS = 16
KV_HEADS = 4
HEAD = 128
PATCH = 128


MASKED = -1e30
LOSS_SCALE = 16.0
EPSILON = 1e-06
MESH = pl.DeviceIdType.MESH
VMEM_SPEC = pl.BlockSpec(memory_space=pltpu.VMEM)


def remote(src, dst, send, recv, axis, peer):
    return pltpu.make_async_remote_copy(
        src_ref=src,
        dst_ref=dst,
        send_sem=send,
        recv_sem=recv,
        device_id={axis: peer},
        device_id_type=MESH,
    )


def greet(axis, peers):
    barrier = pltpu.get_barrier_semaphore()
    for peer in peers:
        pl.semaphore_signal(barrier, inc=1, device_id={axis: peer}, device_id_type=MESH)
    pl.semaphore_wait(barrier, len(peers))


COST = pl.CostEstimate(flops=0, bytes_accessed=24_000_000, transcendentals=0)


def params(collective_id):
    return pltpu.CompilerParams(
        collective_id=collective_id, has_side_effects=True, vmem_limit_bytes=48 * 1024 * 1024
    )


def swap_start(n, src, dst, send, recv):
    me = lax.axis_index("ctx")
    copies = []
    for k in range(1, n):
        peer = lax.rem(me + k, n)
        copy = remote(src.at[peer], dst.at[me], send.at[k - 1], recv.at[k - 1], "ctx", peer)
        copy.start()
        copies.append(copy)
    return copies


def swap_kernel(n, src, dst, send, recv, local):
    me = lax.axis_index("ctx")
    greet("ctx", [lax.rem(me + k, n) for k in range(1, n)])
    copies = swap_start(n, src, dst, send, recv)
    own = pltpu.make_async_copy(src.at[me], dst.at[me], local)
    own.start()
    own.wait()
    for copy in copies:
        copy.wait()


def swap(pieces, n, collective_id):
    return pl.pallas_call(
        functools.partial(swap_kernel, n),
        out_shape=jax.ShapeDtypeStruct(pieces.shape, pieces.dtype),
        in_specs=[VMEM_SPEC],
        out_specs=VMEM_SPEC,
        scratch_shapes=[
            pltpu.SemaphoreType.DMA((n - 1,)),
            pltpu.SemaphoreType.DMA((n - 1,)),
            pltpu.SemaphoreType.DMA,
        ],
        cost_estimate=COST,
        compiler_params=params(collective_id),
    )(pieces)


def front_kernel(
    n,
    dp_n,
    heads,
    query_src,
    key_src,
    value_src,
    weight,
    live,
    dst,
    full,
    attended,
    log_total,
    total,
    product,
    near,
    paired,
    far,
    send,
    recv,
    local,
    up_s,
    dn_s,
    z_r,
    x_s,
    x_r,
    near_s,
    near_r,
    far_s,
    far_r,
):
    me = lax.axis_index("ctx")
    mine = lax.axis_index("dp")
    n_out = dp_n // 2
    outer, inner = mine // 2, lax.rem(mine, 2)
    across = outer * 2 + 1 - inner
    above, below = lax.rem(mine + 2, dp_n), lax.rem(mine + dp_n - 2, dp_n)
    has_up, has_down = outer + 1 < n_out, outer >= 1
    width = weight.shape[1]
    tokens = query_src.shape[0]
    n_ctx = n // 2
    ctx_out, core = me // 2, lax.rem(me, 2)
    partner = ctx_out * 2 + 1 - core
    owners = [lax.rem(ctx_out + k, n_ctx) * 2 for k in range(n_ctx)]

    def columns(index):
        return pl.ds(pl.multiple_of(index * width, width), width)

    def block(index):
        return full.at[:, columns(index)]

    barrier = pltpu.get_barrier_semaphore()
    for k in range(1, n):
        pl.semaphore_signal(
            barrier, inc=1, device_id={"ctx": lax.rem(me + k, n)}, device_id_type=MESH
        )
    for peer in (across, above, below):
        pl.semaphore_signal(barrier, inc=1, device_id={"dp": peer}, device_id_type=MESH)
    pl.semaphore_wait(barrier, n + 2)

    side = jnp.minimum(outer, n_out - 1 - outer)
    origins = [outer]
    for j in range(1, n_out):
        paired_step = (j + 1) // 2
        near_origin = outer - paired_step if j % 2 == 1 else outer + paired_step
        far_origin = jnp.where(outer > n_out - 1 - outer, outer - (j - side), outer + (j - side))
        origins.append(jnp.where(j <= 2 * side, near_origin, far_origin))

    def up(j):
        at = origins[j]
        source = weight if j == 0 else block(at * 2 + inner)
        return remote(source, block(at * 2 + inner), up_s.at[at], z_r.at[at], "dp", above)

    def down(j):
        at = origins[j]
        source = weight if j == 0 else block(at * 2 + inner)
        return remote(source, block(at * 2 + inner), dn_s.at[at], z_r.at[at], "dp", below)

    def cross(j):
        at = origins[j]
        source = weight if j == 0 else block(at * 2 + inner)
        return remote(source, block(at * 2 + inner), x_s.at[at], x_r.at[at], "dp", across)

    def goes_up(j):
        return has_up if j == 0 else jnp.logical_and(has_up, origins[j] < outer)

    def goes_down(j):
        return has_down if j == 0 else jnp.logical_and(has_down, origins[j] > outer)

    own_weight = pltpu.make_async_copy(weight, block(mine), local.at[1])

    def acquire(kind, j):
        if kind == "x":
            cross(j).wait_recv()
            return origins[j] * 2 + 1 - inner
        if j:
            up(j).wait_recv()
        pl.when(goes_up(j))(lambda: up(j).start())
        pl.when(goes_down(j))(lambda: down(j).start())
        cross(j).start()
        if j == 0:
            own_weight.start()
            own_weight.wait()
        return origins[j] * 2 + inner

    span = heads * HEAD
    per_group = HEADS // KV_HEADS

    def parts(owner):
        at = pl.ds(pl.multiple_of(owner * span, HEAD), span)
        head = pl.ds(pl.multiple_of(((owner * heads) // per_group) * HEAD, HEAD), HEAD)
        return [
            (query_src.at[:, at], dst.at[me, :, pl.ds(0, span)]),
            (key_src.at[:, head], dst.at[me, :, pl.ds(span, HEAD)]),
            (value_src.at[:, head], dst.at[me, :, pl.ds(span + HEAD, HEAD)]),
        ]

    copies = []
    for k in range(1, n):
        peer = lax.rem(me + k, n)
        for i, (source, target) in enumerate(parts(peer)):
            copy = remote(source, target, send.at[k - 1, i], recv.at[k - 1, i], "ctx", peer)
            copy.start()
            copies.append(copy)
    owns = []
    for i, (source, target) in enumerate(parts(me)):
        owns.append(pltpu.make_async_copy(source, target, local.at[2 + i]))
        owns[-1].start()
    slots = [("z", 0)]
    for j in range(1, n_out):
        slots += [("z", j), ("x", j - 1)]
    slots.append(("x", n_out - 1))
    positions = [acquire(*slots[0])]
    for copy in owns + copies:
        copy.wait()

    sequence = n * tokens
    keys = dst[:, :, heads * HEAD : (heads + 1) * HEAD].reshape(sequence, HEAD)
    values = dst[:, :, (heads + 1) * HEAD :].reshape(sequence, HEAD)
    is_live = live[...] > 0.5
    group = min(n, 4)
    pieces = [(h, r) for h in range(heads) for r in range(0, n, group)]
    for step, (h, r) in enumerate(pieces):
        at = slice(r * tokens, (r + group) * tokens)
        queries = dst[r : r + group, :, h * HEAD : (h + 1) * HEAD].reshape(group * tokens, HEAD)
        scores = lax.dot_general(
            queries, keys, (((1,), (1,)), ((), ())), preferred_element_type=jnp.float32
        ) / math.sqrt(HEAD)
        scores = jnp.where(is_live, scores, MASKED)
        highest = jnp.max(scores, axis=-1, keepdims=True)
        weights_rows = jnp.exp(scores - highest)
        denominator = jnp.sum(weights_rows, axis=-1, keepdims=True)
        numerator = jnp.dot(
            weights_rows.astype(jnp.bfloat16), values, preferred_element_type=jnp.float32
        )
        attended[at, h * HEAD : (h + 1) * HEAD] = (numerator / denominator).astype(jnp.bfloat16)
        log_total[at, h : h + 1] = highest + jnp.log(denominator)
        if step == len(pieces) // 2 - 1:
            positions.append(acquire(*slots[1]))

    def near_copy(t, k):
        source = product.at[t, owners[k] + 1 - core]
        return remote(source, near.at[t, k], near_s.at[t, k], near_r.at[t, k], "ctx", partner)

    def far_copy(t, k):
        return remote(
            paired.at[t, k - 1],
            far.at[t, k - 1],
            far_s.at[t, k - 1],
            far_r.at[t, k - 1],
            "ctx",
            owners[k] + core,
        )

    def pair(t):
        for k in range(1, n_ctx):
            near_copy(t, k).wait_recv()
            paired[t, k - 1] = (
                product[t, owners[k] + core].astype(jnp.float32) + near[t, k].astype(jnp.float32)
            ).astype(jnp.bfloat16)
            far_copy(t, k).start()

    for t, slot in enumerate(slots):
        if t >= len(positions):
            positions.append(acquire(*slot))
        part = jnp.dot(
            attended[...], full[:, columns(positions[t])], preferred_element_type=jnp.float32
        )
        product[t] = part.astype(jnp.bfloat16).reshape(n, tokens, width)
        for k in list(range(1, n_ctx)) + [0]:
            near_copy(t, k).start()
        if t:
            pair(t - 1)
    pair(len(slots) - 1)
    for t in range(len(slots)):
        near_copy(t, 0).wait_recv()
        whole = product[t, me].astype(jnp.float32) + near[t, 0].astype(jnp.float32)
        for k in range(1, n_ctx):
            far_copy(t, k).wait_recv()
            whole = whole + far[t, k - 1].astype(jnp.float32)
        total[:, columns(positions[t])] = whole

    for j in range(n_out):
        pl.when(goes_up(j))(lambda: up(j).wait_send())
        pl.when(goes_down(j))(lambda: down(j).wait_send())
        cross(j).wait_send()
    for t in range(len(slots)):
        for k in range(n_ctx):
            near_copy(t, k).wait_send()
        for k in range(1, n_ctx):
            far_copy(t, k).wait_send()


def front(queries, keys, values, weight, live, n, dp_n, heads, collective_id):
    dma = pltpu.SemaphoreType.DMA
    n_out, n_ctx = dp_n // 2, n // 2
    tokens = queries.shape[0]
    rows, width = weight.shape
    part = (tokens, width)
    half = jnp.bfloat16
    return pl.pallas_call(
        functools.partial(front_kernel, n, dp_n, heads),
        out_shape=(
            jax.ShapeDtypeStruct((n, tokens, (heads + 2) * HEAD), half),
            jax.ShapeDtypeStruct((rows, width * dp_n), weight.dtype),
            jax.ShapeDtypeStruct((n * tokens, heads * HEAD), half),
            jax.ShapeDtypeStruct((n * tokens, heads), jnp.float32),
            jax.ShapeDtypeStruct((tokens, width * dp_n), jnp.float32),
        ),
        in_specs=[pl.BlockSpec(memory_space=pl.ANY)] * 3 + [VMEM_SPEC] * 2,
        out_specs=(VMEM_SPEC,) * 5,
        scratch_shapes=[
            pltpu.VMEM((dp_n, n) + part, half),
            pltpu.VMEM((dp_n, n_ctx) + part, half),
            pltpu.VMEM((dp_n, n_ctx - 1) + part, half),
            pltpu.VMEM((dp_n, n_ctx - 1) + part, half),
            dma((n - 1, 3)),
            dma((n - 1, 3)),
            dma((5,)),
        ]
        + [dma((n_out,))] * 5
        + [dma((dp_n, n_ctx))] * 2
        + [dma((dp_n, n_ctx - 1))] * 2,
        cost_estimate=COST,
        compiler_params=params(collective_id),
    )(queries, keys, values, weight, live)


def collect_kernel(n, src, dst, send, recv, local):
    me = lax.axis_index("ctx")
    n_out = n // 2
    outer, core = me // 2, lax.rem(me, 2)
    partner = outer * 2 + 1 - core
    peers = [lax.rem(outer + k, n_out) * 2 + core for k in range(1, n_out)]
    greet("ctx", peers + [partner])
    copies = []
    for k, peer in enumerate(peers):
        copy = remote(src, dst.at[me], send.at[k + 1], recv.at[k + 1], "ctx", peer)
        copy.start()
        copies.append(copy)
    first = remote(src, dst.at[me], send.at[0], recv.at[0], "ctx", partner)
    first.start()
    own = pltpu.make_async_copy(src, dst.at[me], local)
    own.start()
    relays = []
    for k, copy in enumerate(copies):
        copy.wait_recv()
        held = lax.rem(outer + n_out - k - 1, n_out) * 2 + core
        relay = remote(
            dst.at[held], dst.at[held], send.at[n_out + k], recv.at[n_out + k], "ctx", partner
        )
        relay.start()
        relays.append(relay)
    own.wait()
    first.wait()
    for copy in copies:
        copy.wait_send()
    for relay in relays:
        relay.wait()


def collect(piece, n, collective_id):
    return pl.pallas_call(
        functools.partial(collect_kernel, n),
        out_shape=jax.ShapeDtypeStruct((n,) + piece.shape, piece.dtype),
        in_specs=[VMEM_SPEC],
        out_specs=VMEM_SPEC,
        scratch_shapes=[
            pltpu.SemaphoreType.DMA((n,)),
            pltpu.SemaphoreType.DMA((n,)),
            pltpu.SemaphoreType.DMA,
        ],
        cost_estimate=COST,
        compiler_params=params(collective_id),
    )(piece)


def reduce_kernel(n, src, dst, near, paired, far, near_s, near_r, far_s, far_r):
    me = lax.axis_index("ctx")
    n_out = n // 2
    outer, core = me // 2, lax.rem(me, 2)
    partner = outer * 2 + 1 - core
    rows = dst.shape[0]
    chunk = 16
    owners = [lax.rem(outer + k, n_out) for k in range(n_out)]
    greet("ctx", [owner * 2 + core for owner in owners[1:]] + [partner])
    nears = {}
    for k in list(range(1, n_out)) + [0]:
        copy = remote(
            src.at[owners[k] * 2 + 1 - core],
            near.at[k],
            near_s.at[k],
            near_r.at[k],
            "ctx",
            partner,
        )
        copy.start()
        nears[k] = copy
    fars = []
    for k in range(1, n_out):
        nears[k].wait_recv()
        source = owners[k] * 2 + core

        @pl.loop(0, rows // chunk)
        def _(r):
            at = pl.ds(pl.multiple_of(r * chunk, chunk), chunk)
            total = src[source, at, :].astype(jnp.float32) + near[k, at, :].astype(jnp.float32)
            paired[k - 1, at, :] = total.astype(jnp.bfloat16)

        copy = remote(
            paired.at[k - 1], far.at[k - 1], far_s.at[k - 1], far_r.at[k - 1], "ctx", source
        )
        copy.start()
        fars.append(copy)
    nears[0].wait_recv()
    for copy in fars:
        copy.wait_recv()

    @pl.loop(0, rows // chunk)
    def _(r):
        at = pl.ds(pl.multiple_of(r * chunk, chunk), chunk)
        total = src[me, at, :].astype(jnp.float32) + near[0, at, :].astype(jnp.float32)
        for k in range(n_out - 1):
            total = total + far[k, at, :].astype(jnp.float32)
        dst[at, :] = total

    for k in range(n_out):
        nears[k].wait_send()
    for copy in fars:
        copy.wait_send()


def reduce(pieces, n, collective_id):
    shape = pieces.shape[1:]
    n_out = n // 2
    dma = pltpu.SemaphoreType.DMA
    return pl.pallas_call(
        functools.partial(reduce_kernel, n),
        out_shape=jax.ShapeDtypeStruct(shape, jnp.float32),
        in_specs=[VMEM_SPEC],
        out_specs=VMEM_SPEC,
        scratch_shapes=[
            pltpu.VMEM((n_out,) + shape, jnp.bfloat16),
            pltpu.VMEM((n_out - 1,) + shape, jnp.bfloat16),
            pltpu.VMEM((n_out - 1,) + shape, jnp.bfloat16),
            dma((n_out,)),
            dma((n_out,)),
            dma((n_out - 1,)),
            dma((n_out - 1,)),
        ],
        cost_estimate=COST,
        compiler_params=params(collective_id),
    )(pieces)


def plan(noise_step):
    phase = (noise_step.astype(jnp.float32) / 1000.0 + 0.008) / 1.008 * (math.pi / 2.0)
    signal_root = jnp.cos(phase)
    return (signal_root, jnp.sqrt(1.0 - signal_root * signal_root))


def gelu_slope(hidden, upstream):
    return jax.vjp(lambda argument: jax.nn.gelu(argument, approximate=True), hidden)[1](upstream)[0]


def matmul(subscripts, left, right):
    return jnp.einsum(subscripts, left, right, preferred_element_type=jnp.float32)


def per_device(
    n,
    dp_n,
    stream,
    queries,
    keys,
    values,
    clip_lengths,
    mod_shift,
    mod_scale,
    out_weight,
    final_weight,
    noisy_latents,
    timestep,
    crop_map,
    embed_weight,
    pre_gain,
    up_weight,
    down_weight,
    post_gain,
    head_weight,
):
    tokens = queries.shape[1]
    sequence = tokens * n
    width = stream.shape[2]
    heads = HEADS // n
    me = lax.axis_index("ctx")
    clip_length = clip_lengths[0]

    is_live = jnp.arange(sequence, dtype=jnp.int32) < clip_length
    swapped, weight, attended, log_total, product = front(
        queries[0],
        keys[0],
        values[0],
        out_weight,
        is_live.astype(jnp.float32)[None],
        n,
        dp_n,
        heads,
        0,
    )
    swapped = swapped.reshape(sequence, (heads + 2) * HEAD)
    query_heads = swapped[:, : heads * HEAD].reshape(sequence, heads, HEAD)
    key_rows = swapped[:, heads * HEAD : (heads + 1) * HEAD]
    value_rows = swapped[:, (heads + 1) * HEAD :]

    residual = stream[0].astype(jnp.float32) + product
    centred = residual - jnp.mean(residual, axis=-1, keepdims=True)
    inverse = lax.rsqrt(jnp.mean(centred * centred, axis=-1, keepdims=True) + EPSILON)
    unit_rows = centred * inverse
    gain_rows = 1.0 + mod_scale[0]
    modulated = (unit_rows * gain_rows + mod_shift[0]).astype(jnp.bfloat16)
    predicted = jnp.dot(modulated, final_weight, preferred_element_type=jnp.float32)
    signal_root, noise_root = plan(timestep[0])
    denoised = (
        (noisy_latents[0].astype(jnp.float32) - noise_root * predicted) / signal_root
    ).astype(jnp.bfloat16)

    final_wide = final_weight.astype(jnp.float32)
    gained = final_wide * gain_rows[:, None]
    gained_mean = jnp.mean(gained, axis=0)
    along_unit = predicted - jnp.sum(final_wide * mod_shift[0][:, None], axis=0)
    bundle = jnp.concatenate(
        [
            denoised,
            along_unit.astype(jnp.bfloat16),
            jnp.broadcast_to(inverse, (tokens, PATCH)).astype(jnp.bfloat16),
        ],
        axis=-1,
    )
    bundles = collect(bundle, n, 2).reshape(sequence, 3 * PATCH)
    gathered = bundles[:, :PATCH]
    n_out = n // 2
    unit_half = unit_rows.astype(jnp.bfloat16)
    to_partner = [(c, c + 1 - 2 * (c % 2)) for c in range(n)]
    held = [(me, unit_half)]
    fars = []
    for k in range(1, n_out):
        moved = lax.ppermute(unit_half, "ctx", [(c, (c + 2 * k) % n) for c in range(n)])
        fars.append((lax.rem(me + n - 2 * k, n), moved))
    beside = lax.ppermute(unit_half, "ctx", to_partner)
    swap_core = 1 - 2 * lax.rem(me, 2)
    gained_out = matmul("rc,cp->rp", weight, gained.astype(jnp.bfloat16)).astype(jnp.bfloat16)
    weight_sum = jnp.sum(weight.astype(jnp.float32), axis=-1)

    crop_rows = crop_map[0]
    crop_tokens = jnp.take(gathered, crop_rows, axis=0)
    embedded = jnp.dot(crop_tokens, embed_weight, preferred_element_type=jnp.float32)
    first_root = jnp.sqrt(jnp.mean(embedded * embedded, axis=-1, keepdims=True) + EPSILON)
    first_unit = embedded / first_root
    normed = (first_unit * pre_gain).astype(jnp.bfloat16)
    hidden = jnp.dot(normed, up_weight, preferred_element_type=jnp.float32)
    active = jax.nn.gelu(hidden, approximate=True).astype(jnp.bfloat16)
    row_total, reward_width = embedded.shape
    rows = row_total // n

    def own_rows(whole):
        return lax.dynamic_slice_in_dim(whole, me * rows, rows, 0)

    head_slope = -(LOSS_SCALE / row_total) * head_weight * post_gain
    down_part = jnp.dot(active, down_weight, preferred_element_type=jnp.float32)
    summed = own_rows(embedded) + reduce(
        down_part.astype(jnp.bfloat16).reshape(n, rows, reward_width), n, 3
    )
    second_root = jnp.sqrt(jnp.mean(summed * summed, axis=-1, keepdims=True) + EPSILON)
    second_unit = summed / second_root
    row_rewards = jnp.sum(second_unit * post_gain * head_weight, axis=-1, keepdims=True)
    summed_slope = (
        head_slope - second_unit * jnp.mean(head_slope * second_unit, axis=-1, keepdims=True)
    ) / second_root
    slope_half, beside, moved = lax.optimization_barrier(
        (summed_slope.astype(jnp.bfloat16), beside, [piece for _, piece in fars])
    )
    relays = [lax.ppermute(piece, "ctx", to_partner) for piece in moved]
    summed_slopes = collect(slope_half, n, 4).reshape(
        row_total, reward_width
    )
    active_slope = matmul("rw,hw->rh", summed_slopes, down_weight)
    hidden_slope = gelu_slope(hidden, active_slope).astype(jnp.bfloat16)
    up_part = matmul("rh,wh->rw", hidden_slope, up_weight)
    normed_slope = (
        reduce(up_part.astype(jnp.bfloat16).reshape(n, rows, reward_width), n, 5) * pre_gain
    )
    own_unit = own_rows(first_unit)
    embed_slope = (
        summed_slope
        + (normed_slope - own_unit * jnp.mean(normed_slope * own_unit, axis=-1, keepdims=True))
        / own_rows(first_root)
    )
    token_slope = matmul("rw,pw->rp", embed_slope.astype(jnp.bfloat16), embed_weight)
    token_slope, relays = lax.optimization_barrier((token_slope, relays))
    token_slopes = collect(
        jnp.concatenate([token_slope, jnp.broadcast_to(row_rewards, (rows, PATCH))], axis=-1), n, 6
    ).reshape(row_total, 2 * PATCH)
    reward = jnp.mean(token_slopes[:, PATCH])
    latent_full = (
        jnp.zeros((sequence, PATCH), jnp.float32).at[crop_rows].add(token_slopes[:, :PATCH])
    )
    noise_slopes = (-(noise_root / signal_root) * latent_full).astype(jnp.bfloat16)
    noise_slope = lax.dynamic_slice_in_dim(noise_slopes, me * tokens, tokens, 0)
    modulated_slope = matmul("tp,dp->td", noise_slope, final_weight) * gain_rows
    residual_slope = (
        modulated_slope
        - jnp.mean(modulated_slope, axis=-1, keepdims=True)
        - unit_rows * jnp.mean(modulated_slope * unit_rows, axis=-1, keepdims=True)
    ) * inverse
    grad_stream = residual_slope.astype(jnp.bfloat16)

    held += [(me + swap_core, beside)]
    for (owner, _), piece, relay in zip(fars, moved, relays):
        held += [(owner, piece), (owner + swap_core, relay)]
    unit_out = jnp.zeros((n, tokens, out_weight.shape[0]), jnp.float32)
    for owner, piece in held:
        part = matmul("tc,rc->tr", piece, weight)
        unit_out = lax.dynamic_update_slice_in_dim(unit_out, part[None], owner, 0)
    unit_out = unit_out.reshape(sequence, out_weight.shape[0])

    noise_wide = noise_slopes.astype(jnp.float32)
    slope_mean = jnp.sum(noise_wide * gained_mean, axis=-1, keepdims=True)
    slope_along = (
        jnp.sum(
            noise_wide * bundles[:, PATCH : 2 * PATCH].astype(jnp.float32), axis=-1, keepdims=True
        )
        / width
    )
    attended_slope = (
        (
            matmul("tp,rp->tr", noise_slopes, gained_out)
            - slope_mean * weight_sum
            - slope_along * unit_out
        )
        * bundles[:, 2 * PATCH : 2 * PATCH + 1].astype(jnp.float32)
    ).astype(jnp.bfloat16)
    slope_heads = attended_slope.reshape(sequence, heads, HEAD)
    row_delta = jnp.sum(
        slope_heads.astype(jnp.float32)
        * attended.reshape(sequence, heads, HEAD).astype(jnp.float32),
        axis=-1,
    ).T
    back_scores = matmul("thd,sd->hts", query_heads, key_rows) / math.sqrt(HEAD)
    back_scores = jnp.where(is_live, back_scores, MASKED)
    back_weights = jnp.exp(back_scores - log_total.T[..., None])
    slopes = matmul("thd,sd->hts", slope_heads, value_rows)
    score_slope = (back_weights * (slopes - row_delta[..., None])).astype(jnp.bfloat16)
    query_slope = matmul("hts,sd->htd", score_slope, key_rows) / math.sqrt(HEAD)
    by_head = (
        jnp.transpose(query_slope, (1, 0, 2))
        .reshape(n, tokens, heads * HEAD)
        .astype(jnp.bfloat16)
    )
    grad_queries = jnp.transpose(swap(by_head, n, 7), (1, 0, 2)).reshape(tokens, HEADS * HEAD)
    return (jnp.reshape(reward, (1,)), grad_stream[None], grad_queries[None])


def solution(mesh):
    return jax.shard_map(
        functools.partial(per_device, mesh.shape["ctx"], mesh.shape["dp"]),
        mesh=mesh,
        in_specs=(
            P("dp", "ctx", None),
            P("dp", "ctx", None),
            P("dp", "ctx", None),
            P("dp", "ctx", None),
            P("dp"),
            P("dp", None),
            P("dp", None),
            P("ctx", "dp"),
            P(),
            P("dp", "ctx", None),
            P("dp"),
            P("dp", None),
            P(),
            P(),
            P(None, "ctx"),
            P("ctx", None),
            P(),
            P(),
        ),
        out_specs=(P("dp"), P("dp", "ctx", None), P("dp", "ctx", None)),
        check_vma=False,
    )
```
